32 devices in a mesh: arow: 4 (over z), acol: 8 (over y, x, core).
Axes of the slice: x: 2, y: 2, z: 4, core: 2. Of those that a mesh axis runs over, the one named last changes fastest.
Arguments:
- row_data: bfloat16 [65536, 128], P(('arow', 'acol')), may hold values from -96 to 96
- row_baseline: int32 [65536], P(('arow', 'acol')), may hold values from 0 to 131071, as said below
- pair_table: int32 [131072, 2], P(('arow', 'acol')), may hold values from 0 to 2047, as said below
- lengths: int32 [131072], P(('arow', 'acol')), may hold values from 1 to 8
- model_vis: bfloat16 [2048, 2048, 128], P('arow', 'acol'), may hold values from -6 to 6
- gains: float32 [2048, 128], P(('arow', 'acol')), may hold values from -6 to 6
Outputs:
- new_gains: float32 [2048, 128], P(('arow', 'acol'))
The draws below stay inside these ranges and needn't reach their ends.
Inputs may be any that keep to these rules, and one draw needn't show every extreme that they name: `pair_table`: slot j belongs to tile o = j // 4096; its first antenna lies in 512 * (o // 8) to 512 * (o // 8 + 1) - 1, its second in 256 * (o % 8) to 256 * (o % 8 + 1) - 1, and the two differ. `row_baseline`: the rows of one device name slots of one tile at most 256 times; one tile is named exactly 256 times by the rows of every device.
All inputs are finite; a program needn't handle non-finite values.
Results may differ from the reference program's by a relative error of at most 0.0003.
Values may be sent and summed in bfloat16 or wider, within the bound.
No kernel may reach another device: no remote copies, remote signals or barrier semaphores. Data moves between devices by JAX's collectives and lax.ppermute only.
A program may use at most 128 MiB of HBM per device.

```python
import jax
import jax.numpy as jnp
from jax import lax

A = 2048
F = 64
ROWS_DEV = 2048
BPO = 4096
AR = 512
AC = 256
CAP = 256
ROWS = 65536
NBW = 131072
DEVICES = 32


def draw_pair_table(key, part):
    index = jnp.arange(NBW, dtype=jnp.int32)
    owner = index // BPO
    blocks = A // AC
    first = owner // blocks * AR + jax.random.randint(jax.random.fold_in(key, 11), (NBW,), 0, AR, dtype=jnp.int32)
    pick = jax.random.randint(jax.random.fold_in(key, 12), (NBW,), 0, AC, dtype=jnp.int32)
    second = owner % blocks * AC + pick
    second = jnp.where(second == first, owner % blocks * AC + (pick + 1) % AC, second)
    return jnp.stack([first, second], axis=1)


def draw_row_baseline(key, part):
    spots = jnp.arange(ROWS_DEV, dtype=jnp.int32)
    flips = jax.random.randint(jax.random.fold_in(key, 21), (DEVICES, ROWS_DEV), 0, 2, dtype=jnp.int32)
    rest = spots[None, :] - CAP
    ranking = jnp.where(spots[None, :] < CAP, 0, 1 + (rest % (DEVICES - 1) + flips) % (DEVICES - 1))
    streams = jax.random.split(jax.random.fold_in(key, 22), DEVICES)
    mixed = jax.vmap(lambda stream, row: row[jax.random.permutation(stream, ROWS_DEV)])(streams, ranking)
    chosen = jax.random.permutation(jax.random.fold_in(key, 23), DEVICES).astype(jnp.int32)
    owner = chosen[mixed]
    pick = jax.random.randint(jax.random.fold_in(key, 24), (DEVICES, ROWS_DEV), 0, BPO, dtype=jnp.int32)
    return (owner * BPO + pick).reshape(ROWS).astype(jnp.int32)


def set_ends(result, stream_key, low, high):
    longest = result.shape.index(max(result.shape))
    spots = []
    for shift in (0, 1):
        where = [jax.random.randint(jax.random.fold_in(stream_key, axis), (), 0, length) for axis, length in enumerate(result.shape)]
        where[longest] = (where[longest] + shift) % result.shape[longest]
        spots.append(tuple(where))
    return result.at[spots[0]].set(low).at[spots[1]].set(high)


def levels(stream_key, shape, cuts, smallest, high):
    gain = 1.0
    for axis_at, shards_of in cuts:
        heights = jax.random.uniform(jax.random.fold_in(jax.random.fold_in(stream_key, 6), axis_at), (shards_of,), jnp.float32, smallest / len(cuts), high / len(cuts))
        gain = gain * jnp.repeat(jnp.exp(heights), shape[axis_at] // shards_of).reshape((-1,) + (1,) * (len(shape) - 1 - axis_at))
    return gain


def noise(stream_key, extent, spread, bound, pieces=(), held_as=jnp.bfloat16):
    entries = jax.random.normal(stream_key, extent, jnp.float32) * spread
    if len(pieces) > 0:
        entries = levels(stream_key, extent, pieces, -0.22, 0.18) * entries
    return jnp.clip(entries, min=-bound, max=bound).astype(held_as)


def setup_inputs(seed: int = 0) -> dict:
    streams_of = jax.random.split(jax.random.key(seed), 7)
    return {
        "row_data": noise(streams_of[0], (ROWS, 2 * F), 16.0, 96.0, ((0, 32),)),
        "row_baseline": draw_row_baseline(jax.random.fold_in(streams_of[6], 71), 0),
        "pair_table": draw_pair_table(jax.random.fold_in(streams_of[6], 71), 0),
        "lengths": set_ends(jax.random.randint(streams_of[3], (NBW,), 1, 9), jax.random.fold_in(streams_of[3], 1), 1, 8).astype(jnp.int32),
        "model_vis": noise(streams_of[4], (A, A, 2 * F), 1.0, 6.0, ((0, 4), (1, 8))),
        "gains": noise(streams_of[5], (A, 2 * F), 1.0, 6.0, ((0, 32),), jnp.float32),
    }


def reference(row_data, row_baseline, pair_table, lengths, model_vis, gains):
    pairs = pair_table[row_baseline]
    first = pairs[:, 0]
    second = pairs[:, 1]
    weight = lengths[row_baseline].astype(jnp.float32)
    terms = weight[:, None] * row_data.astype(jnp.float32)
    nant = gains.shape[0]
    half = gains.shape[1] // 2
    band = nant // 8
    g_re = gains[None, :, :half]
    g_im = gains[None, :, half:]

    def block(index):
        start = index * band
        local = first - start
        inside = (local >= 0) & (local < band)
        spot = jnp.where(inside, local * nant + second, band * nant)
        sums = jnp.zeros((band * nant + 1, 2 * half), jnp.float32).at[spot].add(terms)
        sums = sums[:-1].reshape(band, nant, 2 * half)
        totals = jnp.zeros((band * nant + 1,), jnp.float32).at[spot].add(weight)
        totals = totals[:-1].reshape(band, nant)
        model = lax.dynamic_slice_in_dim(model_vis, start, band, 0)
        m_re = model[..., :half].astype(jnp.float32)
        m_im = model[..., half:].astype(jnp.float32)
        c_re = m_re * g_re + m_im * g_im
        c_im = m_re * g_im - m_im * g_re
        s_re = sums[..., :half]
        s_im = sums[..., half:]
        num = jnp.concatenate([jnp.sum(c_re * s_re - c_im * s_im, axis=1), jnp.sum(c_re * s_im + c_im * s_re, axis=1)], axis=1)
        den = jnp.sum(totals[:, :, None] * (c_re * c_re + c_im * c_im), axis=1)
        return num, den

    nums, dens = lax.map(block, jnp.arange(8, dtype=jnp.int32))
    num = nums.reshape(nant, 2 * half)
    den = dens.reshape(nant, half)
    return jnp.concatenate([num[:, :half] / (den + 1.0), num[:, half:] / (den + 1.0)], axis=1)
```

```python
import math

import jax
import jax.numpy as jnp
from jax import lax
from jax.experimental import pallas as pl
from jax.experimental.pallas import tpu as pltpu
from jax.sharding import PartitionSpec as P

RIDGE = 1.0
BIG = 60 * 1024 * 1024


def pack_kernel(target, local_id, rows, out, tags, wide, placed):
    count = rows.shape[0]
    wide[...] = rows[...].astype(jnp.float32)
    placed[...] = jnp.zeros(placed.shape, jnp.float32)

    def step(i, carry):
        for j in range(16):
            r = i * 16 + j
            t = target[r]
            tags[t] = local_id[r]
            placed[pl.ds(t, 1), :] = wide[pl.ds(r, 1), :]
        return carry

    lax.fori_loop(0, count // 16, step, 0)
    out[...] = placed[...].astype(jnp.bfloat16)


def model_kernel(key, second, gains, model, out, held, sems):
    chunks = sems.shape[0]
    part = held.shape[0] // chunks
    slots = out.shape[0]

    def copy(i):
        return pltpu.make_async_copy(
            model.at[pl.ds(i * part, part)], held.at[pl.ds(i * part, part)], sems.at[i]
        )

    for i in range(chunks):
        copy(i).start()
    width = out.shape[1]
    sub = lax.broadcasted_iota(jnp.int32, (8, width), 0)

    def gain_step(i, carry):
        acc = jnp.zeros((8, width), jnp.float32)
        for j in range(8):
            q = second[i * 8 + j]
            acc = jnp.where(sub == j, gains[pl.ds(q, 1), :], acc)
        out[pl.ds(pl.multiple_of(i * 8, 8), 8), :] = acc
        return carry

    lax.fori_loop(0, slots // 8, gain_step, 0, unroll=2)
    for i in range(chunks):
        copy(i).wait()
    left = lax.broadcasted_iota(jnp.int32, (8, width), 1) < width // 2

    def step(i, carry):
        m = jnp.zeros((8, width), jnp.float32)
        for j in range(8):
            k = key[i * 8 + j]
            tile = held[k // 8].astype(jnp.float32)
            m = jnp.where(sub == j, pltpu.roll(tile, (j - k) & 7, 0), m)
        at = pl.ds(pl.multiple_of(i * 8, 8), 8)
        g = out[at, :]
        a = m * g
        b = m * pltpu.roll(g, width // 2, 1)
        c_re = a + pltpu.roll(a, width // 2, 1)
        c_im = pltpu.roll(b, width // 2, 1) - b
        out[at, :] = jnp.where(left, c_re, c_im)
        return carry

    lax.fori_loop(0, slots // 8, step, 0, unroll=2)


def sum_kernel(high, low, first, lengths, arrived, c, out, wide):
    total, width = arrived.shape
    slots = c.shape[0]
    group = 256
    span = math.gcd(slots, 512)
    row_block = out.shape[0]
    step_k = math.gcd(total, 1024)
    wide[:, :width] = arrived[...]
    wide[:, width:] = jnp.ones((total, width), jnp.bfloat16)
    out[...] = jnp.zeros(out.shape, jnp.float32)
    left = lax.broadcasted_iota(jnp.int32, (span, width), 1) < width // 2

    def step(t, carry):
        acc = jnp.zeros((span, 2 * width), jnp.float32)
        spots = lax.broadcasted_iota(jnp.int32, (group, step_k), 0).astype(jnp.float32).astype(jnp.bfloat16)
        one = jnp.ones((group, step_k), jnp.bfloat16)
        nil = jnp.zeros((group, step_k), jnp.bfloat16)
        for k in range(total // step_k):
            at = pl.ds(k * step_k, step_k)
            hits = []
            for h in range(span // group):
                mine = jnp.where(high[:, at] == t * (span // group) + h, low[:, at], -1.0)
                mine = jnp.broadcast_to(mine.astype(jnp.bfloat16), (group, step_k))
                hits.append(jnp.where(spots == mine, one, nil))
            acc = acc + jnp.dot(
                jnp.concatenate(hits, axis=0), wide[at, :], preferred_element_type=jnp.float32
            )
        s = acc[:, :width]
        w = acc[:, width:]
        base = pl.multiple_of(t * span, span)
        x = c[pl.ds(base, span), :]
        y = pltpu.roll(x, width // 2, 1)
        c_re = jnp.where(left, x, y)
        c_im = jnp.where(left, y, -x)
        num = c_re * s - c_im * pltpu.roll(s, width // 2, 1)
        den = w * (c_re * c_re + c_im * c_im)
        values = jnp.concatenate([num, den], axis=1)
        ants = lax.broadcasted_iota(jnp.int32, (row_block, span), 0)
        pick = jnp.where(
            ants == first[:, pl.ds(base, span)], lengths[:, pl.ds(base, span)].astype(jnp.float32), 0.0
        ).astype(jnp.bfloat16)
        part = jnp.zeros(out.shape, jnp.float32)
        for _ in range(3):
            piece = values.astype(jnp.bfloat16)
            values = values - piece.astype(jnp.float32)
            part = part + jnp.dot(pick, piece, preferred_element_type=jnp.float32)
        out[...] += part
        return carry

    lax.fori_loop(0, slots // span, step, 0)


def column_gains_of(gains, row_count, col_count, my_row):
    got = []
    for m in range(row_count):
        pairs = []
        for col in range(col_count):
            for row in range(row_count):
                pairs.append((col * row_count + (m + row) % row_count, row * col_count + col))
        got.append(lax.ppermute(gains, ("arow", "acol"), pairs))
    stacked = jnp.concatenate(got + got, axis=0)
    height = gains.shape[0]
    start = (row_count - my_row) % row_count * height
    return lax.dynamic_slice_in_dim(stacked, start, row_count * height, 0)


def local(row_data, row_baseline, pair_table, lengths, model_vis, gains):
    row_count = lax.axis_size("arow")
    col_count = lax.axis_size("acol")
    devices = row_count * col_count
    count_rows, width = row_data.shape
    slots = lengths.shape[0]
    capacity = 4 * count_rows // devices
    total = devices * capacity
    row_block, col_block = model_vis.shape[:2]
    my_row = lax.axis_index("arow")
    my_col = lax.axis_index("acol")
    column_gains = column_gains_of(gains, row_count, col_count, my_row)

    owner = row_baseline // slots
    local_id = row_baseline - owner * slots
    hits = (owner[:, None] == jnp.arange(devices, dtype=jnp.int32)[None, :]).astype(jnp.bfloat16)
    step_rows = math.gcd(count_rows, 128)
    blocks = hits.reshape(count_rows // step_rows, step_rows, devices)
    positions = jnp.arange(step_rows, dtype=jnp.int32)
    lower = (positions[:, None] > positions[None, :]).astype(jnp.bfloat16)
    within = jnp.einsum("ij,bjd->bid", lower, blocks, preferred_element_type=jnp.float32)
    per_block = jnp.sum(blocks, axis=1, dtype=jnp.float32)
    before = jnp.cumsum(per_block, axis=0) - per_block
    ranking = jnp.sum(
        (within + before[:, None, :]) * blocks.astype(jnp.float32), axis=2
    ).reshape(count_rows)
    counts = jnp.sum(per_block, axis=0).astype(jnp.int32)
    target = owner * capacity + ranking.astype(jnp.int32)

    smem = pl.BlockSpec(memory_space=pltpu.SMEM)
    vmem = pl.BlockSpec(memory_space=pltpu.VMEM)
    outgoing, tags = pl.pallas_call(
        pack_kernel,
        in_specs=[smem, smem, vmem],
        out_specs=[vmem, smem],
        out_shape=[
            jax.ShapeDtypeStruct((total, width), jnp.bfloat16),
            jax.ShapeDtypeStruct((total,), jnp.int32),
        ],
        scratch_shapes=[
            pltpu.VMEM((count_rows, width), jnp.float32),
            pltpu.VMEM((total, width), jnp.float32),
        ],
        compiler_params=pltpu.CompilerParams(vmem_limit_bytes=BIG),
        name="pack",
    )(target, local_id, row_data)
    labels = jnp.where(
        jnp.arange(capacity, dtype=jnp.int32)[None, :] < counts[:, None],
        tags.reshape(devices, capacity),
        -1,
    )
    names = lax.all_to_all(labels, ("arow", "acol"), split_axis=0, concat_axis=0, tiled=True)
    arrived = lax.all_to_all(
        outgoing.reshape(devices, capacity, width),
        ("arow", "acol"),
        split_axis=0,
        concat_axis=0,
        tiled=True,
    ).reshape(total, width)

    first = jnp.clip(pair_table[:, 0] - my_row * row_block, 0, row_block - 1)
    second = jnp.clip(pair_table[:, 1] - my_col * col_block, 0, col_block - 1)
    tiles = row_block * col_block // 8
    chunks = math.gcd(tiles, 8)
    c = pl.pallas_call(
        model_kernel,
        in_specs=[smem, smem, vmem, pl.BlockSpec(memory_space=pl.ANY)],
        out_specs=vmem,
        out_shape=jax.ShapeDtypeStruct((slots, width), jnp.float32),
        scratch_shapes=[
            pltpu.VMEM((tiles, 8, width), jnp.bfloat16),
            pltpu.SemaphoreType.DMA((chunks,)),
        ],
        compiler_params=pltpu.CompilerParams(vmem_limit_bytes=BIG),
        name="model",
    )(first * col_block + second, second, column_gains, model_vis.reshape(tiles, 8, width))

    names = names.reshape(1, total)
    high = names >> 8
    low = (names & 255).astype(jnp.float32)
    sums = pl.pallas_call(
        sum_kernel,
        in_specs=[vmem] * 6,
        out_specs=vmem,
        out_shape=jax.ShapeDtypeStruct((row_block, 2 * width), jnp.float32),
        scratch_shapes=[pltpu.VMEM((total, 2 * width), jnp.bfloat16)],
        compiler_params=pltpu.CompilerParams(vmem_limit_bytes=BIG),
        name="sums",
    )(high, low, first.reshape(1, slots), lengths.reshape(1, slots), arrived, c)
    share = row_block // col_count
    parts = lax.all_to_all(
        sums.reshape(col_count, share, 2 * width), "acol", split_axis=0, concat_axis=0, tiled=True
    )
    whole = jnp.sum(parts, axis=0)
    return whole[:, :width] / (whole[:, width:] + RIDGE)


def solution(mesh):
    placed = (
        P(("arow", "acol"), None),
        P(("arow", "acol")),
        P(("arow", "acol"), None),
        P(("arow", "acol")),
        P("arow", "acol", None),
        P(("arow", "acol"), None),
    )
    return jax.shard_map(
        local, mesh=mesh, in_specs=placed, out_specs=P(("arow", "acol"), None), check_vma=False
    )
```

```python
import math

import jax
import jax.numpy as jnp
from jax import lax
from jax.experimental import pallas as pl
from jax.experimental.pallas import tpu as pltpu
from jax.sharding import PartitionSpec as P

RIDGE = 1.0
BIG = 60 * 1024 * 1024


def pack_kernel(target, local_id, rows, out, tags, wide, placed):
    count = rows.shape[0]
    wide[...] = rows[...].astype(jnp.float32)
    placed[...] = jnp.zeros(placed.shape, jnp.float32)

    def step(i, carry):
        for j in range(16):
            r = i * 16 + j
            t = target[r]
            tags[t] = local_id[r]
            placed[pl.ds(t, 1), :] = wide[pl.ds(r, 1), :]
        return carry

    lax.fori_loop(0, count // 16, step, 0)
    out[...] = placed[...].astype(jnp.bfloat16)


def model_kernel(key, model, out, held, sems):
    chunks = sems.shape[0]
    part = held.shape[0] // chunks
    slots, width = out.shape

    def copy(i):
        return pltpu.make_async_copy(
            model.at[pl.ds(i * part, part)], held.at[pl.ds(i * part, part)], sems.at[i]
        )

    for i in range(chunks):
        copy(i).start()
    sub = lax.broadcasted_iota(jnp.int32, (8, width), 0)
    for i in range(chunks):
        copy(i).wait()

    def step(i, carry):
        for g in range(4):
            base = pl.multiple_of(i * 32 + g * 8, 8)
            m = jnp.zeros((8, width), jnp.float32)
            for j in range(8):
                k = key[base + j]
                tile = held[k >> 3].astype(jnp.float32)
                m = jnp.where(sub == j, pltpu.roll(tile, (j - k) & 7, 0), m)
            out[pl.ds(base, 8), :] = m
        return carry

    lax.fori_loop(0, slots // 32, step, 0)


def sum_kernel(high, low, first, second, lengths, arrived, model, gains, out, wide, pieces):
    total, width = arrived.shape
    slots = model.shape[0]
    col_block = gains.shape[0]
    group = 256
    span = math.gcd(slots, 512)
    row_block = out.shape[0]
    step_k = math.gcd(total, 1024)
    wide[:, :width] = arrived[...]
    wide[:, width:] = jnp.ones((total, width), jnp.bfloat16)
    out[...] = jnp.zeros(out.shape, jnp.float32)
    rest = gains[...]
    for i in range(3):
        piece = rest.astype(jnp.bfloat16)
        rest = rest - piece.astype(jnp.float32)
        pieces[:, i * width : (i + 1) * width] = piece

    def step(t, carry):
        acc = jnp.zeros((span, 2 * width), jnp.float32)
        spots = lax.broadcasted_iota(jnp.int32, (group, step_k), 0).astype(jnp.float32).astype(jnp.bfloat16)
        one = jnp.ones((group, step_k), jnp.bfloat16)
        nil = jnp.zeros((group, step_k), jnp.bfloat16)
        for k in range(total // step_k):
            at = pl.ds(k * step_k, step_k)
            hits = []
            for h in range(span // group):
                mine = jnp.where(high[:, at] == t * (span // group) + h, low[:, at], -1.0)
                mine = jnp.broadcast_to(mine.astype(jnp.bfloat16), (group, step_k))
                hits.append(jnp.where(spots == mine, one, nil))
            acc = acc + jnp.dot(
                jnp.concatenate(hits, axis=0), wide[at, :], preferred_element_type=jnp.float32
            )
        s = acc[:, :width]
        w = acc[:, width:]
        base = pl.multiple_of(t * span, span)
        cols = lax.broadcasted_iota(jnp.int32, (col_block, span), 0)
        choose = jnp.where(cols == second[:, pl.ds(base, span)], 1.0, 0.0).astype(jnp.bfloat16)
        g3 = lax.dot_general(
            choose, pieces[...], (((0,), (0,)), ((), ())), preferred_element_type=jnp.float32
        )
        g = g3[:, :width] + g3[:, width : 2 * width] + g3[:, 2 * width :]
        m = model[pl.ds(base, span), :]
        a = m * g
        b = m * pltpu.roll(g, width // 2, 1)
        c_re = a + pltpu.roll(a, width // 2, 1)
        c_im = b - pltpu.roll(b, width // 2, 1)
        num = c_re * s - c_im * pltpu.roll(s, width // 2, 1)
        den = w * (c_re * c_re + c_im * c_im)
        values = jnp.concatenate([num, den], axis=1)
        ants = lax.broadcasted_iota(jnp.int32, (row_block, span), 0)
        pick = jnp.where(
            ants == first[:, pl.ds(base, span)], lengths[:, pl.ds(base, span)].astype(jnp.float32), 0.0
        ).astype(jnp.bfloat16)
        part = jnp.zeros(out.shape, jnp.float32)
        for _ in range(3):
            piece = values.astype(jnp.bfloat16)
            values = values - piece.astype(jnp.float32)
            part = part + jnp.dot(pick, piece, preferred_element_type=jnp.float32)
        out[...] += part
        return carry

    lax.fori_loop(0, slots // span, step, 0)


def column_gains_of(gains, row_count, col_count, my_row):
    got = []
    for m in range(row_count):
        pairs = []
        for col in range(col_count):
            for row in range(row_count):
                pairs.append((col * row_count + (m + row) % row_count, row * col_count + col))
        got.append(lax.ppermute(gains, ("arow", "acol"), pairs))
    stacked = jnp.concatenate(got + got, axis=0)
    height = gains.shape[0]
    start = (row_count - my_row) % row_count * height
    return lax.dynamic_slice_in_dim(stacked, start, row_count * height, 0)


def local(row_data, row_baseline, pair_table, lengths, model_vis, gains):
    row_count = lax.axis_size("arow")
    col_count = lax.axis_size("acol")
    devices = row_count * col_count
    count_rows, width = row_data.shape
    slots = lengths.shape[0]
    capacity = 4 * count_rows // devices
    extra = -(-2 * capacity // (16 * width)) * 16
    stride = capacity + extra
    total = devices * stride
    row_block, col_block = model_vis.shape[:2]
    my_row = lax.axis_index("arow")
    my_col = lax.axis_index("acol")
    column_gains = column_gains_of(gains, row_count, col_count, my_row)

    owner = row_baseline // slots
    local_id = row_baseline - owner * slots
    hits = (owner[:, None] == jnp.arange(devices, dtype=jnp.int32)[None, :]).astype(jnp.bfloat16)
    step_rows = math.gcd(count_rows, 128)
    blocks = hits.reshape(count_rows // step_rows, step_rows, devices)
    positions = jnp.arange(step_rows, dtype=jnp.int32)
    lower = (positions[:, None] > positions[None, :]).astype(jnp.bfloat16)
    within = jnp.einsum("ij,bjd->bid", lower, blocks, preferred_element_type=jnp.float32)
    per_block = jnp.sum(blocks, axis=1, dtype=jnp.float32)
    before = jnp.cumsum(per_block, axis=0) - per_block
    ranking = jnp.sum(
        (within + before[:, None, :]) * blocks.astype(jnp.float32), axis=2
    ).reshape(count_rows)
    counts = jnp.sum(per_block, axis=0).astype(jnp.int32)
    target = owner * stride + ranking.astype(jnp.int32)

    smem = pl.BlockSpec(memory_space=pltpu.SMEM)
    vmem = pl.BlockSpec(memory_space=pltpu.VMEM)
    outgoing, tags = pl.pallas_call(
        pack_kernel,
        in_specs=[smem, smem, vmem],
        out_specs=[vmem, smem],
        out_shape=[
            jax.ShapeDtypeStruct((total, width), jnp.bfloat16),
            jax.ShapeDtypeStruct((total,), jnp.int32),
        ],
        scratch_shapes=[
            pltpu.VMEM((count_rows, width), jnp.float32),
            pltpu.VMEM((total, width), jnp.float32),
        ],
        compiler_params=pltpu.CompilerParams(vmem_limit_bytes=BIG),
        name="pack",
    )(target, local_id, row_data)
    tags = tags.reshape(devices, stride)[:, :capacity]
    valid = jnp.arange(capacity, dtype=jnp.int32)[None, :] < counts[:, None]
    marks = jnp.concatenate(
        [jnp.where(valid, (tags >> 8) + 1, 0), jnp.where(valid, tags & 255, 0)], axis=1
    ).astype(jnp.bfloat16)
    marks = jnp.pad(marks, ((0, 0), (0, extra * width - 2 * capacity)))
    outgoing = lax.dynamic_update_slice(
        outgoing.reshape(devices, stride, width), marks.reshape(devices, extra, width), (0, capacity, 0)
    )
    arrived = lax.all_to_all(
        outgoing, ("arow", "acol"), split_axis=0, concat_axis=0, tiled=True
    )
    marks = arrived[:, capacity:, :].reshape(devices, extra * width).astype(jnp.float32)
    arrived = arrived.reshape(total, width)

    first = jnp.clip(pair_table[:, 0] - my_row * row_block, 0, row_block - 1)
    second = jnp.clip(pair_table[:, 1] - my_col * col_block, 0, col_block - 1)
    tiles = row_block * col_block // 8
    chunks = math.gcd(tiles, 8)
    model_rows = pl.pallas_call(
        model_kernel,
        in_specs=[smem, pl.BlockSpec(memory_space=pl.ANY)],
        out_specs=vmem,
        out_shape=jax.ShapeDtypeStruct((slots, width), jnp.float32),
        scratch_shapes=[
            pltpu.VMEM((tiles, 8, width), jnp.bfloat16),
            pltpu.SemaphoreType.DMA((chunks,)),
        ],
        compiler_params=pltpu.CompilerParams(vmem_limit_bytes=BIG),
        name="model",
    )(first * col_block + second, model_vis.reshape(tiles, 8, width))

    room = ((0, 0), (0, extra))
    high = jnp.pad(marks[:, :capacity].astype(jnp.int32) - 1, room, constant_values=-1)
    low = jnp.pad(marks[:, capacity : 2 * capacity], room)
    high = high.reshape(1, total)
    low = low.reshape(1, total)
    sums = pl.pallas_call(
        sum_kernel,
        in_specs=[vmem] * 8,
        out_specs=vmem,
        out_shape=jax.ShapeDtypeStruct((row_block, 2 * width), jnp.float32),
        scratch_shapes=[
            pltpu.VMEM((total, 2 * width), jnp.bfloat16),
            pltpu.VMEM((col_block, 3 * width), jnp.bfloat16),
        ],
        compiler_params=pltpu.CompilerParams(vmem_limit_bytes=BIG),
        name="sums",
    )(
        high,
        low,
        first.reshape(1, slots),
        second.reshape(1, slots),
        lengths.reshape(1, slots),
        arrived,
        model_rows,
        column_gains,
    )
    share = row_block // col_count
    parts = lax.all_to_all(
        sums.reshape(col_count, share, 2 * width), "acol", split_axis=0, concat_axis=0, tiled=True
    )
    whole = jnp.sum(parts, axis=0)
    return whole[:, :width] / (whole[:, width:] + RIDGE)


def solution(mesh):
    placed = (
        P(("arow", "acol"), None),
        P(("arow", "acol")),
        P(("arow", "acol"), None),
        P(("arow", "acol")),
        P("arow", "acol", None),
        P(("arow", "acol"), None),
    )
    return jax.shard_map(
        local, mesh=mesh, in_specs=placed, out_specs=P(("arow", "acol"), None), check_vma=False
    )
```
